32 devices in a mesh: grp: 8 (over y, x, core), blk: 4 (over z).
Axes of the slice: x: 2, y: 2, z: 4, core: 2. Of those that a mesh axis runs over, the one named last changes fastest.
Arguments:
- a_blocks: bfloat16 [1024, 24, 4096], P(('grp', 'blk')), may hold values from -0.25 to 0.25
- a_cols: int32 [1024, 24], P(('grp', 'blk')), may hold values from 0 to 127, as said below
- p_blocks: bfloat16 [1024, 3, 4096], P(('grp', 'blk')), may hold values from -1 to 1
- p_cols: int32 [1024, 3], P('grp'), may hold values from 0 to 31, as said below
- owner: int32 [4, 8, 8], P('blk'), may hold values from 0 to 7, as said below
Outputs:
- coarse_out: bfloat16 [256, 11, 4096], P(('grp', 'blk'))
The draws below stay inside these ranges and needn't reach their ends.
Inputs may be any that keep to these rules, and one draw needn't show every extreme that they name: `a_cols`: the first block of each fine row is its diagonal block; every other block's row has an aggregate at cyclic distance at most 1 from the row's aggregate over the group's 32 aggregates; a column may repeat, and repeated blocks add. `p_cols`: the first block of each fine row is its aggregate; the group's fine rows b * 32 to (b + 1) * 32 - 1 hold exactly the aggregates b * 8 to (b + 1) * 8 - 1, 4 rows each; the other two are distinct aggregates at cyclic distance 1 or 2 from it. `owner`: for each blk index and group, the 8 coarse rows go to distinct grp indices.
All inputs are finite; a program needn't handle non-finite values.
Results may differ from the reference program's by a relative error of at most 0.0053.
Values may be sent and summed in bfloat16 or wider, within the bound.
No kernel may reach another device: no remote copies, remote signals or barrier semaphores. Data moves between devices by JAX's collectives and lax.ppermute only.
A program may use at most 128 MiB of HBM per device.

```python
import jax
import jax.numpy as jnp
import numpy as np
from jax import lax

B = 64
BC = 64
KA = 24
KP = 3
RATIO = 4
SPREAD = 7
BAND = 11
NB = 32
NCD = 8
FG = 128
NC = 32
N_GRP = 8
N_BLK = 4


def group_layout(key):
    keys = jax.random.split(jax.random.fold_in(key, 11), N_GRP * N_BLK)
    local = jax.vmap(lambda single: jax.random.permutation(single, NB))(keys).astype(jnp.int32)
    base = (jnp.arange(N_BLK, dtype=jnp.int32) * NB)[None, :, None]
    places = (local.reshape(N_GRP, N_BLK, NB) + base).reshape(N_GRP, FG).astype(jnp.int32)
    inverse = jnp.argsort(places, axis=1, stable=True).astype(jnp.int32)
    return (places, inverse)


def draw_p_cols(key, part):
    places, inverse = group_layout(key)
    aggregate = places // RATIO
    pairs = jnp.array(np.array([[-2, -1], [-2, 1], [-2, 2], [-1, 1], [-1, 2], [1, 2]], dtype=np.int32))
    choose = jax.random.randint(jax.random.fold_in(key, 23), (N_GRP, FG), 0, 6)
    offsets = pairs[choose]
    first = (aggregate + offsets[..., 0]) % NC
    second = (aggregate + offsets[..., 1]) % NC
    result = jnp.stack([aggregate, first, second], axis=-1)
    return result.reshape(N_GRP * FG, 3).astype(jnp.int32)


def draw_a_cols(key, part):
    places, inverse = group_layout(key)
    aggregate = places // RATIO
    steps_near = jax.random.randint(jax.random.fold_in(key, 31), (N_GRP, FG, KA - 1), -1, 2)
    members = jax.random.randint(jax.random.fold_in(key, 37), (N_GRP, FG, KA - 1), 0, RATIO)
    target_place = (aggregate[:, :, None] + steps_near) % NC * RATIO + members
    rows_far = jax.vmap(lambda table, wanted: table[wanted])(inverse, target_place)
    own_rows = jnp.broadcast_to(jnp.arange(FG, dtype=jnp.int32)[None, :, None], (N_GRP, FG, 1))
    result = jnp.concatenate([own_rows, rows_far.astype(jnp.int32)], axis=-1)
    return result.reshape(N_GRP * FG, KA).astype(jnp.int32)


def draw_owner(key, part):
    keys = jax.random.split(jax.random.fold_in(key, 41), N_BLK * N_GRP)
    orders = jax.vmap(lambda single: jax.random.permutation(single, N_GRP))(keys).astype(jnp.int32)
    return orders[:, :NCD].reshape(N_BLK, N_GRP, NCD)


def shard_levels(key, extent, cuts, smallest, top_value):
    factor_of, own = 1.0, jax.random.fold_in(key, 6)
    for dim, blocks in cuts:
        draws = jnp.exp(jax.random.uniform(jax.random.fold_in(own, dim), (blocks,), jnp.float32, smallest / len(cuts), top_value / len(cuts)))
        factor_of = factor_of * jnp.repeat(draws, extent[dim] // blocks).reshape([-1 if axis == dim else 1 for axis in range(len(extent))])
    return factor_of


def scatter_about(key, dims, spread, limit, cuts=(), held_as=jnp.bfloat16):
    values = jax.random.normal(key, dims, jnp.float32) * spread
    if len(cuts) > 0:
        values = shard_levels(key, dims, cuts, -0.22, 0.18) * values
    return jnp.clip(values, min=-limit, max=limit).astype(held_as)


def setup_inputs(seed: int = 0) -> dict:
    streams_of = jax.random.split(jax.random.key(seed), 6)
    a_blocks = scatter_about(streams_of[0], (N_GRP * FG, KA, B * B), (KA * B * KP // 7) ** -0.5, 0.25, ((0, 32),))
    a_cols = draw_a_cols(jax.random.fold_in(streams_of[5], 71), 0)
    p_blocks = scatter_about(streams_of[2], (N_GRP * FG, KP, B * BC), (B // 2) ** -0.5, 1.0, ((0, 32),))
    p_cols = draw_p_cols(jax.random.fold_in(streams_of[5], 71), 0)
    owner = draw_owner(jax.random.fold_in(streams_of[5], 71), 0)
    return dict(a_blocks=a_blocks, a_cols=a_cols, p_blocks=p_blocks, p_cols=p_cols, owner=owner)


def cyclic(value, modulus):
    return (value + modulus // 2) % modulus - modulus // 2


def device_term(group_p, group_cols, a_part, col_part, p_part, own_cols):
    aggregate = own_cols[:, 0]
    picked = group_p[col_part].astype(jnp.float32).reshape(NB, KA, KP, B, BC)
    far_cols = group_cols[col_part]
    slot_ids = cyclic(far_cols - aggregate[:, None, None], NC) + SPREAD // 2
    onehot = (slot_ids[..., None] == jnp.arange(SPREAD, dtype=jnp.int32)).astype(jnp.float32)
    products = jnp.einsum("fkab,fkmbc->fkmac", a_part.astype(jnp.float32).reshape(NB, KA, B, B), picked,
                          precision=lax.Precision.HIGHEST)
    ap_rows = jnp.einsum("fkmac,fkme->feac", products, onehot,
                         precision=lax.Precision.HIGHEST).astype(jnp.bfloat16)
    blocks_out = jnp.einsum("frbc,febd->frecd", p_part.astype(jnp.float32).reshape(NB, KP, B, BC),
                            ap_rows.astype(jnp.float32), precision=lax.Precision.HIGHEST)
    shifts = jnp.arange(SPREAD, dtype=jnp.int32) - SPREAD // 2
    band_ids = cyclic(aggregate[:, None, None] + shifts[None, None, :] - own_cols[:, :, None], NC) + BAND // 2
    targets = own_cols[:, :, None] * BAND + band_ids
    summed = jax.ops.segment_sum(blocks_out.reshape(-1, BC * BC), targets.reshape(-1), num_segments=NC * BAND)
    rounded = lax.optimization_barrier(summed.astype(jnp.bfloat16))
    return rounded.astype(jnp.float32)


def group_coarse(pieces):
    a_group, col_group, p_group, pcol_group = pieces
    items = (a_group.reshape(N_BLK, NB, KA, B * B), col_group.reshape(N_BLK, NB, KA),
             p_group.reshape(N_BLK, NB, KP, B * BC), pcol_group.reshape(N_BLK, NB, KP))

    def advance(running, item):
        a_part, col_part, p_part, own_cols = item
        return running + device_term(p_group, pcol_group, a_part, col_part, p_part, own_cols), None

    running, _ = lax.scan(advance, jnp.zeros((NC * BAND, BC * BC), jnp.float32), items)
    return running.astype(jnp.bfloat16).reshape(NC, BAND, BC * BC)


def reference(a_blocks, a_cols, p_blocks, p_cols, owner):
    coarse = lax.map(group_coarse, (a_blocks.reshape(N_GRP, FG, KA, B * B), a_cols.reshape(N_GRP, FG, KA),
                                    p_blocks.reshape(N_GRP, FG, KP, B * BC), p_cols.reshape(N_GRP, FG, KP)))
    by_place = jnp.transpose(coarse.reshape(N_GRP, N_BLK, NCD, BAND, BC * BC), (1, 0, 2, 3, 4))

    def for_owner(owner_index):
        owned = owner == owner_index
        chosen = jnp.where(owned[..., None, None], by_place, jnp.zeros((), jnp.bfloat16))
        return jnp.sum(chosen.astype(jnp.float32), axis=2).astype(jnp.bfloat16)

    result = lax.map(for_owner, jnp.arange(N_GRP, dtype=jnp.int32))
    return result.reshape(N_GRP * N_BLK * N_GRP, BAND, BC * BC)
```

```python
import functools

import jax
import jax.numpy as jnp
from jax import lax
from jax.experimental import pallas as pl
from jax.experimental.pallas import tpu as pltpu
from jax.sharding import PartitionSpec as P

RATIO = 4
REACH = 2
F32 = jnp.float32
BF16 = jnp.bfloat16
LIMIT = 40 * 1024 * 1024


def iota(shape, axis):
    return lax.broadcasted_iota(jnp.int32, shape, axis)


def rows_sum(values):
    return jnp.sum(values.astype(F32), axis=0, keepdims=True)


def lanes_sum(values):
    return jnp.sum(values.astype(F32), axis=1, keepdims=True)


def wrapped(values, modulus):
    half = modulus // 2
    values = jnp.where(values >= half, values - modulus, values)
    return jnp.where(values < -half, values + modulus, values)


def places(cols_ref, mine, rows):
    group = cols_ref.shape[1]
    agg_row = cols_ref[0:1, :].astype(F32)
    sub, lane = iota((group, group), 0), iota((group, group), 1)
    agg_wide = jnp.broadcast_to(agg_row, (group, group))
    agg_col = lanes_sum(jnp.where(sub == lane, agg_wide, 0.0))
    same = agg_wide == agg_col
    member_row = rows_sum(jnp.where(same & (sub < lane), 1.0, 0.0))
    member_col = lanes_sum(jnp.where(same & (lane < sub), 1.0, 0.0))
    base = (mine * rows).astype(F32)
    place_row = wrapped(agg_row * RATIO + member_row - base, group)
    place_col = wrapped(agg_col * RATIO + member_col - base, group)
    return place_row, place_col


def column_rel(cols_ref, mine, coarse):
    total = cols_ref.shape[1] // RATIO
    cols = cols_ref[...].astype(F32)
    near = wrapped(cols - cols[0:1, :], total)
    own = wrapped(cols[0:1, :] - (mine * coarse).astype(F32), total)
    return own + near


def own_lanes(values, mine, rows):
    group = values.shape[1]
    values = jnp.broadcast_to(values, (8, group))
    return pltpu.roll(values, (group - mine * rows) % group, 1)[:, :128]


def three_wide(pieces, rows):
    lane = iota((8, 128), 1)
    out = jnp.full((8, 128), -1.0, F32)
    for m, piece in enumerate(pieces):
        moved = piece if m == 0 else pltpu.roll(piece, m * rows, 1)
        out = jnp.where((lane >= m * rows) & (lane < (m + 1) * rows), moved, out)
    return out


def onehot(code, count):
    hit = iota((count, code.shape[1]), 0).astype(F32) == code
    return jnp.where(hit, 1.0, 0.0).astype(BF16)


def dot(a, b):
    return jnp.dot(a, b, preferred_element_type=F32)


def swap_halves(first, second):
    low = iota(first.shape, 1) < 64
    even = jnp.where(low, first, pltpu.roll(second, 64, 1))
    odd = jnp.where(low, pltpu.roll(first, 64, 1), second)
    return even, odd


def send_rows_kernel(cols_ref, p_ref, before_ref, after_ref):
    rows = p_ref.shape[0] // 3
    width = p_ref.shape[1]
    half = width // 2
    mine = lax.axis_index("blk")
    place_row, _ = places(cols_ref, mine, rows)
    place = own_lanes(place_row, mine, rows)
    codes = [[], [], []]
    for first in (0, rows - RATIO):
        member = place - first
        good = (member >= 0) & (member < RATIO)
        none = jnp.full((8, 128), -1.0, F32)
        mem = jnp.where(good, member, none)
        nxt = jnp.where(good, member + RATIO, none)
        codes[0].append(three_wide((mem, nxt, none), rows))
        codes[1].append(three_wide((none, none, mem), rows))
        codes[2].append(three_wide((none, none, nxt), rows))
    picks = [jnp.concatenate([onehot(c[0:1, : 3 * rows], 8) for c in pair], axis=0) for pair in codes]
    left = dot(jnp.concatenate([picks[0], picks[1]], axis=0), p_ref[:, :half])
    right = dot(jnp.concatenate([picks[0], picks[2]], axis=0), p_ref[:, half:])
    for side, ref in ((0, before_ref), (1, after_ref)):
        at = 8 * side
        ref[:, :half] = left[at : at + 8].astype(BF16)
        ref[:, half:width] = right[at : at + 8].astype(BF16)
        ref[:, width:] = (left[16 + at : 24 + at] + right[16 + at : 24 + at]).astype(BF16)


def spread_rows(flat, work_ref, out_ref, row0, count, tile_count):
    per = count * 8
    highs = flat.shape[1] // 128
    for high in range(highs):
        work_ref[high * per : (high + 1) * per, :] = flat[:, high * 128 : (high + 1) * 128]
    for j in range(count):
        for tile in range(tile_count):
            first = work_ref[pl.ds(j * 8 + 2 * tile, highs, stride=per), :]
            second = work_ref[pl.ds(j * 8 + 2 * tile + 1, highs, stride=per), :]
            even, odd = swap_halves(first, second)
            out_ref[tile, pl.ds(row0 + j * 64, highs, stride=2), :] = even
            out_ref[tile, pl.ds(row0 + j * 64 + 1, highs, stride=2), :] = odd


def merge_kernel(smem_cols, cols_ref, acols_ref, p_ref, a_ref, lhs_ref, z_ref, pt_ref, halo_ref,
                 buf, place_smem, count_smem, sel, psel, work, zf, sems):
    rows, ka, width = a_ref.shape
    group = cols_ref.shape[1]
    coarse = rows // RATIO
    quads = rows // 8
    mine = lax.axis_index("blk")

    for c in range(coarse):
        count_smem[c] = 0

    def order(f, carry):
        agg = smem_cols[0, mine * rows + f] - mine * coarse
        at = count_smem[agg]
        count_smem[agg] = at + 1
        pltpu.make_async_copy(a_ref.at[f], buf.at[agg * RATIO + at, pl.ds(0, ka), :], sems.at[agg // 2]).start()
        return carry

    lax.fori_loop(0, rows, order, 0)
    buf[:, ka:, :] = jnp.zeros((rows, 32 - ka, width), BF16)

    place_row, place_col = places(cols_ref, mine, rows)
    col_rel = column_rel(cols_ref, mine, coarse)
    first = ((mine - 1) * rows).astype(F32)

    span = rows * 32
    rel = acols_ref[...].astype(F32) - first
    rel = jnp.where(rel < 0, rel + group, rel)
    rel = jnp.where(rel >= group, rel - group, rel)
    place_smem[...] = jnp.broadcast_to(place_col, (group, 128))
    own_col = place_smem[pl.ds(pl.multiple_of(mine * rows, 8), rows), :][:, 0:1]
    lane_row = iota((rows, span), 1) // 32
    to_lane = jnp.where(own_col == lane_row.astype(F32), 1.0, 0.0).astype(BF16)
    wide = dot(rel.astype(BF16), to_lane)
    k_lane = iota((ka, span), 1) % 32
    far = rows_sum(jnp.where(iota((ka, span), 0) == k_lane, wide, 0.0))
    rel_w = iota((group, 1), 0).astype(F32) - first
    rel_w = jnp.where(rel_w < 0, rel_w + group, rel_w)
    rel_w = jnp.where(rel_w >= group, rel_w - group, rel_w)
    far_place = rows_sum(jnp.where(rel_w == far, place_col, 0.0))
    lane = iota((1, span), 1)
    code = (far_place - (8 * (lane // 256) - RATIO).astype(F32)) * 8 + ((lane // 32) % 8).astype(F32)
    code = jnp.where(lane % 32 < ka, code, -1.0)
    for q in range(quads):
        sel[q] = onehot(code[:, q * 256 : (q + 1) * 256], 128)

    place = own_lanes(place_row, mine, rows).astype(jnp.int32)
    z_codes, t_codes = [], []
    for m in range(3):
        col = own_lanes(col_rel[m : m + 1], mine, rows).astype(jnp.int32)
        pair = (place + RATIO) // 8
        z_codes.append((pair * 64 + (place + RATIO) % 8 * 8 + col + 3 - 2 * pair).astype(F32))
        q = place // 8
        t_codes.append((q * 48 + (col + 2 - 2 * q) * 8 + place % 8).astype(F32))
    z_code = three_wide(z_codes, rows)[0:1, : 3 * rows]
    t_code = three_wide(t_codes, rows)[0:1, : 3 * rows]
    z_pick = onehot(z_code, (quads + 1) * 64)
    psel[...] = onehot(t_code, quads * 48)

    diag = iota((group, group), 0) == iota((group, group), 1)
    col_cols = [lanes_sum(jnp.where(diag, jnp.broadcast_to(col_rel[m : m + 1], (group, group)), 0.0)) for m in range(3)]
    r = iota((1, 16), 1)
    r_m = jnp.where(r < 8, r // RATIO, 2)
    r_i = r % RATIO
    for side, (start, shift) in enumerate(((-RATIO, 3), (rows, 3 - coarse))):
        hit = place_col == (r_i + start).astype(F32)
        slot = jnp.zeros((1, 16), F32)
        for m in range(3):
            slot = jnp.where(r_m == m, rows_sum(jnp.where(hit, col_cols[m], 0.0)), slot)
        row_code = (r_i * 8 + shift).astype(F32) + slot
        for part in range(2):
            keep = (r < 8) | (((r % 8) // RATIO) == part)
            halo_ref[side, part] = onehot(jnp.where(keep, row_code, -1.0), 32)

    for pair in range(quads + 1):
        flat = dot(z_pick[pair * 64 : (pair + 1) * 64], p_ref[...])
        spread_rows(flat, work, zf, 0, 8, 3)
        for tile in range(3):
            z_ref[pair, :, tile * 128 : (tile + 1) * 128] = zf[tile].astype(BF16)

    for q in range(quads):
        for _ in range(8):
            pltpu.make_async_copy(a_ref.at[0], buf.at[0, pl.ds(0, ka), :], sems.at[q]).wait()

        def chunk(step, carry):
            lanes = pl.ds(pl.multiple_of(step * 256, 256), 256)
            source = buf[q * 8 : (q + 1) * 8, :, lanes].reshape(256, 256)
            got = dot(sel[q], source)
            own = dot(psel[q * 48 : (q + 1) * 48, :], p_ref[:, lanes])
            at = pl.multiple_of(step * 16, 16)
            for values, ref, pairs in ((got, lhs_ref, 8), (own, pt_ref, 3)):
                for t in range(pairs):
                    a, b = (
                        jnp.concatenate([values[(2 * t + w) * 8 : (2 * t + w + 1) * 8, h * 128 : (h + 1) * 128]
                                         for h in range(2)], axis=0)
                        for w in range(2)
                    )
                    even, odd = swap_halves(a, b)
                    ref[q, pl.ds(at, 16), t * 128 : (t + 1) * 128] = even.astype(BF16)
                    ref[q, pl.ds(at + 256, 16), t * 128 : (t + 1) * 128] = odd.astype(BF16)
            return carry

        lax.fori_loop(0, width // 256, chunk, 0, unroll=2)


def second_product(pt, ap):
    return lax.dot_general(pt, ap, (((0,), (0,)), ((), ())), preferred_element_type=F32)


def blocks_of(acc_ref, row0, put):
    for tile in range(acc_ref.shape[0]):
        even = acc_ref[tile, pl.ds(row0, 32, stride=2), :]
        odd = acc_ref[tile, pl.ds(row0 + 1, 32, stride=2), :]
        first, second = swap_halves(even, odd)
        put(2 * tile, first)
        put(2 * tile + 1, second)


def edge_kernel(halo_ref, before_ref, after_ref, lhs_ref, z_ref, pt_ref, to_before, to_after, acc_ref,
                work, zf, zb, ap, part):
    quads = pt_ref.shape[0]
    width = before_ref.shape[1] // 3 * 2
    half = width // 2
    last = quads - 1
    band = to_before.shape[0] // 32
    for side, ref in ((0, before_ref), (1, after_ref)):
        pieces = []
        for h in range(2):
            pick = halo_ref[side, h]
            pieces.append(dot(pick[:, 0:8], ref[:, h * half : (h + 1) * half]) + dot(pick[:, 8:16], ref[:, width:]))
        flat = jnp.concatenate(pieces, axis=1)
        spread_rows(flat, work, zf, 0, 4, 3)
        for tile in range(3):
            zb[side, :, tile * 128 : (tile + 1) * 128] = zf[tile].astype(BF16)
    acc_ref[...] = jnp.zeros(acc_ref.shape, F32)
    for side, q in ((0, 0), (1, last)):
        lhs = lhs_ref.at[q]
        for at in range(0, 512, 128):
            rows = slice(at, at + 128)
            if side == 0:
                low = dot(lhs[rows, 0:256], zb[0]) + dot(lhs[rows, 256:512], z_ref[0, 256:512])
                high = dot(lhs[rows, 512:1024], z_ref[1])
            else:
                low = dot(lhs[rows, 0:512], z_ref[last])
                high = dot(lhs[rows, 512:768], z_ref[last + 1, 0:256]) + dot(lhs[rows, 768:1024], zb[1])
            ap[rows, 0:128] = low[:, 0:128].astype(BF16)
            ap[rows, 128:384] = (low[:, 128:] + high[:, :256]).astype(BF16)
            ap[rows, 384:512] = high[:, 256:].astype(BF16)
        product = second_product(pt_ref[q], ap[...])
        for tile in range(4):
            part[tile] = product[:, tile * 128 : (tile + 1) * 128]
        out_ref = (to_before, to_after)[side]
        for n, i in enumerate((0, 1) if side == 0 else (4, 5)):
            slots = range(4 - i, 11) if side == 0 else range(0, 12 - i)
            base = (0, 7)[n] if side == 0 else (0, 8)[n]

            def put(x, block):
                slot = x - i + 4
                if slot in slots:
                    at = (base + slot - slots[0]) * 32
                    out_ref[at : at + 32, :] = block.astype(BF16)

            blocks_of(part, i * 64, put)
        row0, acc0 = (128, 0) if side == 0 else (0, acc_ref.shape[1] - 256)
        acc_ref[q : q + 4, acc0 : acc0 + 256, :] = part[:, row0 : row0 + 256, :]


def inner_kernel(lhs_ref, z_ref, pt_ref, edge_ref, own_ref, acc, ap):
    quads = pt_ref.shape[0]
    coarse = own_ref.shape[0]
    band = own_ref.shape[1] // 32
    acc[...] = edge_ref[...]
    for q in range(1, quads - 1):
        lhs = lhs_ref.at[q]
        for at in range(0, 512, 128):
            rows = slice(at, at + 128)
            low = dot(lhs[rows, 0:512], z_ref[q])
            high = dot(lhs[rows, 512:1024], z_ref[q + 1])
            ap[rows, 0:128] = low[:, 0:128].astype(BF16)
            ap[rows, 128:384] = (low[:, 128:] + high[:, :256]).astype(BF16)
            ap[rows, 384:512] = high[:, 256:].astype(BF16)
        at = (2 * q - 2) * 64
        product = second_product(pt_ref[q], ap[...])
        for tile in range(4):
            acc[q + tile, at : at + 384, :] += product[:, tile * 128 : (tile + 1) * 128]
    for c in range(coarse):
        for slot in (s for s in range(band) if not 0 <= c + s - 2 < acc.shape[0] * 2):
            own_ref[c, slot * 32 : slot * 32 + 32, :] = jnp.zeros((32, 128), BF16)

        def put(x, block):
            slot = x - c + 2
            if 0 <= slot < band:
                own_ref[c, slot * 32 : slot * 32 + 32, :] = block.astype(BF16)

        blocks_of(acc, c * 64, put)


def reduce_kernel(owner_ref, own_ref, before_ref, after_ref, out_ref):
    coarse, rows, _ = own_ref.shape
    me = lax.axis_index("grp")
    count = out_ref.shape[0]
    if count > coarse:
        for h in range(count):
            out_ref[h] = jnp.zeros(out_ref.shape[1:], BF16)
    for c in range(coarse):
        target = owner_ref[0, me, c]
        if c < 2:
            at, size, base = 0, (8 - c) * 32, 8 * 32 * c
            extra = before_ref[base : base + size, :]
        elif c >= coarse - 2:
            n = c - (coarse - 2)
            size, base = (7 + n) * 32, 7 * 32 * n
            at = rows - size
            extra = after_ref[base : base + size, :]
        else:
            size = 0
        if size == 0:
            out_ref[target] = own_ref[c]
            continue
        if at > 0:
            out_ref[target, 0:at, :] = own_ref[c, 0:at, :]
        if at + size < rows:
            out_ref[target, at + size :, :] = own_ref[c, at + size :, :]
        total = own_ref[c, at : at + size, :].astype(F32) + extra.astype(F32)
        out_ref[target, at : at + size, :] = total.astype(BF16)


def place_kernel(in_ref, out_ref, work):
    count, rows, _ = in_ref.shape
    band = rows // 32
    for q in range(count):
        work[q * rows : (q + 1) * rows, :] = in_ref[q].astype(F32)

    def one(s, carry):
        for h in range(32):
            tile = work[pl.ds(s * 32 + h, count, stride=rows), :]
            out_ref[s, :, h * 128 : (h + 1) * 128] = tile.astype(BF16)
        return carry

    lax.fori_loop(0, band, one, 0)


VM = pl.BlockSpec(memory_space=pltpu.VMEM)
SM = pl.BlockSpec(memory_space=pltpu.SMEM)
ANY = pl.BlockSpec(memory_space=pl.ANY)


def call(kernel, outs, ins, scratch=(), flops=0, size=0):
    return pl.pallas_call(
        kernel,
        out_shape=[jax.ShapeDtypeStruct(s, d) for s, d in outs],
        in_specs=ins,
        out_specs=[VM] * len(outs),
        scratch_shapes=list(scratch),
        compiler_params=pltpu.CompilerParams(vmem_limit_bytes=LIMIT),
        cost_estimate=pl.CostEstimate(flops=flops, bytes_accessed=size, transcendentals=0),
    )


def body(a_blocks, a_cols, p_blocks, p_cols, owner):
    rows, ka, width = a_blocks.shape
    group = p_cols.shape[0]
    coarse = rows // RATIO
    quads = rows // 8
    band = 11
    blks, grps = lax.axis_size("blk"), lax.axis_size("grp")
    cols_t = p_cols.T
    acols_t = a_cols.T
    p_flat = jnp.transpose(p_blocks, (1, 0, 2)).reshape(3 * rows, width)
    tail = width // 2 * 3
    to_before, to_after = call(send_rows_kernel, [((8, tail), BF16)] * 2, [VM, VM], size=1 << 20)(cols_t, p_flat)
    up = [(i, (i + 1) % blks) for i in range(blks)]
    down = [((i + 1) % blks, i) for i in range(blks)]
    p_before = lax.ppermute(to_after, "blk", up)
    p_after = lax.ppermute(to_before, "blk", down)
    lhs, z, pt, halo = call(
        merge_kernel,
        [((quads, 512, 1024), BF16), ((quads + 1, 512, 384), BF16), ((quads, 512, 384), BF16), ((2, 2, 32, 16), BF16)],
        [SM, VM, VM, VM, ANY],
        [
            pltpu.VMEM((rows, 32, width), BF16),
            pltpu.VMEM((group, 128), F32),
            pltpu.SMEM((coarse,), jnp.int32),
            pltpu.VMEM((quads, 128, 256), BF16),
            pltpu.VMEM((quads * 48, 3 * rows), BF16),
            pltpu.VMEM((32 * 64, 128), F32),
            pltpu.VMEM((3, 512, 128), F32),
            pltpu.SemaphoreType.DMA((quads,)),
        ],
        flops=4 << 30, size=16 << 20,
    )(cols_t, cols_t, acols_t, p_flat, a_blocks)
    send_before, send_after, edge = call(
        edge_kernel,
        [((15 * 32, 128), BF16)] * 2 + [((quads + 3, coarse * 64, 128), F32)],
        [VM] * 6,
        [
            pltpu.VMEM((32 * 32, 128), F32),
            pltpu.VMEM((3, 256, 128), F32),
            pltpu.VMEM((2, 256, 384), BF16),
            pltpu.VMEM((512, 512), BF16),
            pltpu.VMEM((4, 384, 128), F32),
        ],
        flops=1 << 30, size=4 << 20,
    )(halo, p_before, p_after, lhs, z, pt)
    from_before = lax.ppermute(send_after, "blk", up)
    from_after = lax.ppermute(send_before, "blk", down)
    (own,) = call(
        inner_kernel,
        [((coarse, band * 32, 128), BF16)],
        [VM] * 4,
        [pltpu.VMEM((quads + 3, coarse * 64, 128), F32), pltpu.VMEM((512, 512), BF16)],
        flops=2 << 30, size=8 << 20,
    )(lhs, z, pt, edge)
    (outgoing,) = call(
        reduce_kernel, [((grps, band * 32, 128), BF16)], [SM, VM, VM, VM], size=2 << 20
    )(owner, own, from_before, from_after)
    arrived = lax.all_to_all(outgoing, "grp", split_axis=0, concat_axis=0, tiled=True)
    (placed,) = call(
        place_kernel, [((band, grps, width), BF16)], [VM], [pltpu.VMEM((grps * band * 32, 128), F32)], size=2 << 20
    )(arrived)
    return jnp.transpose(placed, (1, 0, 2))


def solution(mesh):
    return jax.shard_map(
        body,
        mesh=mesh,
        in_specs=(
            P(("grp", "blk"), None, None),
            P(("grp", "blk"), None),
            P(("grp", "blk"), None, None),
            P("grp", None),
            P("blk", None, None),
        ),
        out_specs=P(("grp", "blk"), None, None),
        check_vma=False,
    )
```

```python
import functools

import jax
import jax.numpy as jnp
from jax import lax
from jax.experimental import pallas as pl
from jax.experimental.pallas import tpu as pltpu
from jax.sharding import PartitionSpec as P

RATIO = 4
REACH = 2
F32 = jnp.float32
BF16 = jnp.bfloat16
LIMIT = 40 * 1024 * 1024
CHUNK = 4096
UNROLL = 1
PUNROLL = 4
ZUNROLL = 1


def iota(shape, axis):
    return lax.broadcasted_iota(jnp.int32, shape, axis)


def rows_sum(values):
    return jnp.sum(values.astype(F32), axis=0, keepdims=True)


def wrapped(values, modulus):
    half = modulus // 2
    values = jnp.where(values >= half, values - modulus, values)
    return jnp.where(values < -half, values + modulus, values)


def across(mask, values):
    picked = jnp.where(mask, values, 0.0).astype(BF16)
    return dot(picked, jnp.ones((picked.shape[1], 128), BF16))


def places(cols_ref, mine, rows):
    group = cols_ref.shape[1]
    agg_row = cols_ref[0:1, :].astype(F32)
    sub, lane = iota((group, group), 0), iota((group, group), 1)
    agg_wide = jnp.broadcast_to(agg_row, (group, group))
    agg_col = across(sub == lane, agg_wide)
    same = agg_wide == jnp.concatenate([agg_col] * (group // 128), axis=1)
    member_row = rows_sum(jnp.where(same & (sub < lane), 1.0, 0.0))
    member_col = across(same & (lane < sub), 1.0)
    base = (mine * rows).astype(F32)
    place_row = wrapped(agg_row * RATIO + member_row - base, group)
    place_col = wrapped(agg_col * RATIO + member_col - base, group)
    return place_row, place_col


def column_rel(cols_ref, mine, coarse):
    total = cols_ref.shape[1] // RATIO
    cols = cols_ref[...].astype(F32)
    near = wrapped(cols - cols[0:1, :], total)
    own = wrapped(cols[0:1, :] - (mine * coarse).astype(F32), total)
    return own + near


def own_lanes(values, mine, rows):
    group = values.shape[1]
    values = jnp.broadcast_to(values, (8, group))
    return pltpu.roll(values, (group - mine * rows) % group, 1)[:, :128]


def three_wide(pieces, rows):
    lane = iota((8, 128), 1)
    out = jnp.full((8, 128), -1.0, F32)
    for m, piece in enumerate(pieces):
        moved = piece if m == 0 else pltpu.roll(piece, m * rows, 1)
        out = jnp.where((lane >= m * rows) & (lane < (m + 1) * rows), moved, out)
    return out


def onehot(code, count):
    hit = iota((count, code.shape[1]), 0).astype(F32) == code
    return jnp.where(hit, 1.0, 0.0).astype(BF16)


def dot(a, b):
    return jnp.dot(a, b, preferred_element_type=F32)


def swap_halves(first, second):
    low = iota(first.shape, 1) < 64
    even = jnp.where(low, first, pltpu.roll(second, 64, 1))
    odd = jnp.where(low, pltpu.roll(first, 64, 1), second)
    return even, odd


def fetch(pairs, sems):
    copies = [pltpu.make_async_copy(src, dst, sems.at[n]) for n, (src, dst) in enumerate(pairs)]
    for copy in copies:
        copy.start()
    return copies


def send_rows_kernel(cols_hbm, p_hbm, out_ref, cols_ref, p_ref, sems):
    for copy in fetch(((cols_hbm, cols_ref), (p_hbm, p_ref)), sems):
        copy.wait()
    rows = p_ref.shape[0] // 3
    width = p_ref.shape[1]
    half = width // 2
    mine = lax.axis_index("blk")
    place_row, _ = places(cols_ref, mine, rows)
    place = own_lanes(place_row, mine, rows)
    codes = [[], [], []]
    for first in (0, rows - RATIO):
        member = place - first
        good = (member >= 0) & (member < RATIO)
        none = jnp.full((8, 128), -1.0, F32)
        mem = jnp.where(good, member, none)
        nxt = jnp.where(good, member + RATIO, none)
        codes[0].append(three_wide((mem, nxt, none), rows))
        codes[1].append(three_wide((none, none, mem), rows))
        codes[2].append(three_wide((none, none, nxt), rows))
    picks = [jnp.concatenate([onehot(c[0:1, : 3 * rows], 8) for c in pair], axis=0) for pair in codes]
    left = dot(jnp.concatenate([picks[0], picks[1]], axis=0), p_ref[:, :half])
    right = dot(jnp.concatenate([picks[0], picks[2]], axis=0), p_ref[:, half:])
    odd = mine % 2
    for side in range(2):
        at = 8 * side
        ref = out_ref.at[(side + odd + 1) % 2]
        ref[:, :half] = left[at : at + 8].astype(BF16)
        ref[:, half:width] = right[at : at + 8].astype(BF16)
        ref[:, width:] = (left[16 + at : 24 + at] + right[16 + at : 24 + at]).astype(BF16)


def halves(values):
    low = iota(values.shape, 1) % 128 < 64
    turned = jnp.concatenate(
        [pltpu.roll(values[:, at : at + 128], 64, 1) for at in range(0, values.shape[1], 128)], axis=1
    )
    none = jnp.zeros(values.shape, BF16)
    even = (jnp.where(low, values, none), jnp.where(low, none, turned))
    odd = (jnp.where(low, turned, none), jnp.where(low, none, values))
    return even, odd


def spread_store(flat, work_ref, row, pitch):
    for at in range(0, flat.shape[0], 8):
        work_ref[pl.ds(at * pitch + 2 * row, 8, stride=pitch), :] = flat[at : at + 8]


def spread_load(work_ref, j, pitch, out_ref, lead, at):
    size = pitch // 2 - 1
    for tile in range(3):
        block = work_ref[pl.ds((j * 4 + tile) * pitch, size, stride=2), :]
        out_ref[lead, pl.ds(at, size), tile * 128 : (tile + 1) * 128] = block.astype(BF16)


def unpack(values, ref, lead, at, pairs):
    for t in range(pairs):
        a, b = (
            jnp.concatenate([values[(2 * t + w) * 8 : (2 * t + w + 1) * 8, h * 128 : (h + 1) * 128]
                             for h in range(2)], axis=0).astype(BF16)
            for w in range(2)
        )
        even, odd = swap_halves(a, b)
        ref[lead, pl.ds(at, 16), t * 128 : (t + 1) * 128] = even
        ref[lead, pl.ds(at + 256, 16), t * 128 : (t + 1) * 128] = odd


def combine(low, high, at, put):
    put(at, 0, low[:, 0:128])
    put(at, 128, low[:, 128:] + high[:, :256])
    put(at, 384, high[:, 256:])


def merge_kernel(smem_cols, cols_hbm, acols_hbm, p_hbm, a_ref, lhs_ref, z_ref, pt_ref, halo_ref, base_ref,
                 buf, place_ref, count_smem, order_smem, sel, psel, work, pe, po, cols_ref, acols_ref, p_ref, sems, in_sems):
    rows, ka, width = a_ref.shape
    group = cols_ref.shape[1]
    coarse = rows // RATIO
    quads = rows // 8
    small = fetch(((cols_hbm, cols_ref), (acols_hbm, acols_ref), (p_hbm, p_ref)), in_sems)
    large = fetch([(a_ref.at[pl.ds(q * 8, 8)], buf.at[pl.ds(q * 8, 8)]) for q in range(quads)], sems)
    mine = lax.axis_index("blk")
    for c in range(coarse):
        count_smem[c] = 0
    for f in range(rows):
        agg = smem_cols[0, mine * rows + f] - mine * coarse
        at = count_smem[agg]
        count_smem[agg] = at + 1
        order_smem[agg * RATIO + at] = f
    for copy in small:
        copy.wait()
    p_rows = 3 * rows
    for at in range(0, width, 128):
        lanes = slice(at, at + 128)
        even, odd = halves(p_ref[:, lanes])
        for n in range(2):
            pe[n * p_rows : (n + 1) * p_rows, lanes] = even[n]
            po[n * p_rows : (n + 1) * p_rows, lanes] = odd[n]

    place_row, place_col = places(cols_ref, mine, rows)
    col_rel = column_rel(cols_ref, mine, coarse)
    first = ((mine - 1) * rows).astype(F32)

    step = 8 * ka
    span = quads * 256
    lane = iota((1, span), 1)
    inner = lane % 256
    lane_row = lane // 256 * 8 + inner // ka
    valid = inner < step
    rel = acols_ref[...].astype(F32) - first
    rel = jnp.where(rel < 0, rel + group, rel)
    rel = jnp.where(rel >= group, rel - group, rel)
    place_ref[...] = place_col
    own_col = place_ref[pl.ds(pl.multiple_of(mine * rows, 8), rows), :]
    own_col = jnp.concatenate([own_col] * (span // 128), axis=1)
    to_lane = jnp.where(own_col == jnp.where(valid, lane_row, -1).astype(F32), 1.0, 0.0).astype(BF16)
    wide = dot(rel.astype(BF16), to_lane)
    far = rows_sum(jnp.where(iota((ka, span), 0) == inner % ka, wide, 0.0))
    rel_w = iota((group, 128), 0).astype(F32) - first
    rel_w = jnp.where(rel_w < 0, rel_w + group, rel_w)
    rel_w = jnp.where(rel_w >= group, rel_w - group, rel_w)
    codes = []
    for at in range(0, span, 128):
        far_place = rows_sum(jnp.where(rel_w == far[:, at : at + 128], place_col, 0.0))
        codes.append(far_place)
    code = jnp.concatenate(codes, axis=1)
    code = (code - (8 * (lane // 256) - RATIO).astype(F32)) * 8 + (inner // ka).astype(F32)
    code = jnp.where(valid, code, -1.0)
    for q in range(quads):
        sel[q] = onehot(code[:, q * 256 : q * 256 + step], 128)

    place = own_lanes(place_row, mine, rows).astype(jnp.int32)
    z_rows, t_rows = (quads + 1) * 32, quads * 24
    codes = ([], []), ([], [])
    for m in range(3):
        col = own_lanes(col_rel[m : m + 1], mine, rows).astype(jnp.int32)
        pair, q = (place + RATIO) // 8, place // 8
        slot = col + 3 - 2 * pair
        z_code = pair * 32 + (place + RATIO) % 8 * 4 + slot // 2
        near = col + 2 - 2 * q
        t_code = q * 24 + near // 2 * 8 + place % 8
        for parity in range(2):
            codes[0][parity].append(jnp.where(slot % 2 == parity, z_code, -1).astype(F32))
            codes[1][parity].append(jnp.where(near % 2 == parity, t_code, -1).astype(F32))
    for parity in range(2):
        lanes = slice(parity * p_rows, (parity + 1) * p_rows)
        psel[0:z_rows, lanes] = onehot(three_wide(codes[0][parity], rows)[0:1, :p_rows], z_rows)
        psel[z_rows:, lanes] = onehot(three_wide(codes[1][parity], rows)[0:1, :p_rows], t_rows)

    diag = iota((group, group), 0) == iota((group, group), 1)
    col_cols = [across(diag, jnp.broadcast_to(col_rel[m : m + 1], (group, group)))[:, 0:16] for m in range(3)]
    place_16 = place_col[:, 0:16]
    r = iota((1, 16), 1)
    r_m = jnp.where(r < 8, r // RATIO, 2)
    r_i = r % RATIO
    for side, (start, shift) in enumerate(((-RATIO, 3), (rows, 3 - coarse))):
        hit = place_16 == (r_i + start).astype(F32)
        slot = jnp.zeros((1, 16), F32)
        for m in range(3):
            slot = jnp.where(r_m == m, rows_sum(jnp.where(hit, col_cols[m], 0.0)), slot)
        slot = slot.astype(jnp.int32) + shift
        row_code = r_i * 4 + slot // 2
        for part in range(2):
            keep = (r < 8) | (((r % 8) // RATIO) == part)
            for parity in range(2):
                code = jnp.where(keep & (slot % 2 == parity), row_code, -1).astype(F32)
                halo_ref[side, part, parity] = onehot(code, 16)

    pitch = 2 * (width // 64 + 1)

    def p_chunk(step, carry):
        lanes = pl.ds(pl.multiple_of(step * 256, 256), 256)
        for lo, ref in enumerate((pe, po)):
            picked = dot(psel[...], ref[:, lanes])
            for h in range(2):
                spread_store(picked[:z_rows, h * 128 : (h + 1) * 128], work, step * 4 + 2 * h + lo, pitch)
            for n in range(t_rows // 8):
                q, t = n // 3, n % 3
                rows8 = picked[z_rows + n * 8 : z_rows + n * 8 + 8]
                block = jnp.concatenate([rows8[:, :128], rows8[:, 128:]], axis=0).astype(BF16)
                pt_ref[q, pl.ds(pl.multiple_of(step * 16, 16) + 256 * lo, 16), t * 128 : (t + 1) * 128] = block
        return carry

    lax.fori_loop(0, width // 256, p_chunk, 0, unroll=PUNROLL)

    def z_pair(pair, carry):
        for j in range(8):
            spread_load(work, pair * 8 + j, pitch, z_ref, pair, j * 64)
        return carry

    lax.fori_loop(0, quads + 1, z_pair, 0, unroll=ZUNROLL)
    for copy in large:
        copy.wait()

    def quad(q, carry):
        def chunk(step, carry):
            lanes = pl.ds(pl.multiple_of(step * CHUNK, CHUNK), CHUNK)
            source = jnp.concatenate([buf[order_smem[q * 8 + i], :, lanes] for i in range(8)], axis=0)
            got = dot(sel[q], source)
            for h in range(CHUNK // 256):
                at = pl.multiple_of(step * (CHUNK // 16) + h * 16, 16)
                unpack(got[:, h * 256 : (h + 1) * 256], lhs_ref, q, at, 8)
            return carry

        return lax.fori_loop(0, width // CHUNK, chunk, carry, unroll=UNROLL)

    lax.fori_loop(0, quads, quad, 0)

    last = quads - 1
    for side, q in ((0, 0), (1, last)):

        def put(at, lane, value):
            base_ref[side, at : at + 128, lane : lane + value.shape[1]] = value

        for at in range(0, 512, 128):
            part = slice(at, at + 128)
            if side == 0:
                low = dot(lhs_ref[q, part, 256:512], z_ref[0, 256:512])
                high = dot(lhs_ref[q, part, 512:1024], z_ref[1])
            else:
                low = dot(lhs_ref[q, part, 0:512], z_ref[last])
                high = dot(lhs_ref[q, part, 512:768], z_ref[last + 1, 0:256])
            combine(low, high, at, put)


def second_product(pt, ap):
    return lax.dot_general(pt, ap, (((0,), (0,)), ((), ())), preferred_element_type=F32)


def blocks_of(acc_ref, row0, put):
    for tile in range(acc_ref.shape[0]):
        even = acc_ref[tile, pl.ds(row0, 32, stride=2), :]
        odd = acc_ref[tile, pl.ds(row0 + 1, 32, stride=2), :]
        first, second = swap_halves(even, odd)
        put(2 * tile, first)
        put(2 * tile + 1, second)


def edge_kernel(halo_ref, first_ref, second_ref, lhs_ref, base_ref, pt_ref, out_ref, ap_ref, work, zb, part):
    last = pt_ref.shape[0] - 1
    width = first_ref.shape[1] // 3 * 2
    half = width // 2
    odd = lax.axis_index("blk") % 2
    here = jnp.broadcast_to(odd, (8, 128)) == 0
    for side in range(2):
        def rows_of(lanes):
            one, two = first_ref[:, lanes].astype(F32), second_ref[:, lanes].astype(F32)
            even = jnp.broadcast_to(odd == side, one.shape)
            return jnp.where(even, two, one).astype(BF16)

        pitch = 2 * (width // 64 + 1)
        for h in range(2):
            rows16 = jnp.concatenate([rows_of(slice(h * half, (h + 1) * half)), rows_of(slice(width, None))], axis=0)
            for lo, stacks in enumerate(halves(rows16)):
                picked = dot(halo_ref[side, h, 0], stacks[0]) + dot(halo_ref[side, h, 1], stacks[1])
                for high in range(half // 128):
                    row = 2 * (h * (half // 128) + high) + lo
                    spread_store(picked[:, high * 128 : (high + 1) * 128], work, row, pitch)
        for j in range(4):
            spread_load(work, j, pitch, zb, side, j * 64)
    for side, q in ((0, 0), (1, last)):
        lane, more, lane0 = (0, 0, 0) if side == 0 else (768, 128, 384)
        for at in range(0, 512, 128):
            rows = slice(at, at + 128)
            extra = dot(lhs_ref[q, rows, lane : lane + 256], zb[side])
            ap_ref[side, rows, more : more + 384] = (base_ref[side, rows, more : more + 384] + extra).astype(BF16)
            ap_ref[side, rows, 384 - lane0 : 512 - lane0] = base_ref[side, rows, 384 - lane0 : 512 - lane0].astype(BF16)
        cut = slice(0, 128) if side == 0 else slice(256, 384)
        product = second_product(pt_ref[q, :, cut], ap_ref[side])
        for tile in range(4):
            part[tile] = product[:, tile * 128 : (tile + 1) * 128]
        target = out_ref.at[(side + odd + 1) % 2]
        for n, i in enumerate((0, 1) if side == 0 else (4, 5)):
            slots = range(4 - i, 11) if side == 0 else range(0, 12 - i)
            base = (0, 7)[n] if side == 0 else (0, 8)[n]

            def put(x, block):
                slot = x - i + 4
                if slot in slots:
                    at = (base + slot - slots[0]) * 32
                    target[at : at + 32, :] = block.astype(BF16)

            blocks_of(part, n * 64, put)


def inner_kernel(lhs_ref, z_ref, pt_ref, edge_ref, own_ref, acc, ap):
    quads = pt_ref.shape[0]
    coarse = own_ref.shape[0]
    band = own_ref.shape[1] // 32
    acc[...] = jnp.zeros(acc.shape, F32)
    for q in range(quads):
        if q == 0:
            product, at = second_product(pt_ref[q, :, 128:384], edge_ref[0]), 0
        elif q == quads - 1:
            product, at = second_product(pt_ref[q, :, 0:256], edge_ref[1]), acc.shape[1] - 256
        else:

            def put(at, lane, value):
                ap[at : at + 128, lane : lane + value.shape[1]] = value.astype(BF16)

            for at in range(0, 512, 128):
                rows = slice(at, at + 128)
                low = dot(lhs_ref[q, rows, 0:512], z_ref[q])
                high = dot(lhs_ref[q, rows, 512:1024], z_ref[q + 1])
                combine(low, high, at, put)
            product, at = second_product(pt_ref[q], ap[...]), (2 * q - 2) * 64
        for tile in range(4):
            acc[q + tile, at : at + product.shape[0], :] += product[:, tile * 128 : (tile + 1) * 128]
    for c in range(coarse):
        for slot in (s for s in range(band) if not 0 <= c + s - 2 < acc.shape[0] * 2):
            own_ref[c, slot * 32 : slot * 32 + 32, :] = jnp.zeros((32, 128), BF16)

        def put(x, block):
            slot = x - c + 2
            if 0 <= slot < band:
                own_ref[c, slot * 32 : slot * 32 + 32, :] = block.astype(BF16)

        blocks_of(acc, c * 64, put)


def reduce_kernel(owner_ref, own_ref, first_ref, second_ref, *refs):
    out_refs, full = refs[:-1], refs[-1]
    coarse, rows, _ = own_ref.shape
    me = lax.axis_index("grp")
    odd = lax.axis_index("blk") % 2
    for c in range(coarse):
        if c < 2:
            at, size, base, side = 0, (8 - c) * 32, 8 * 32 * c, 0
        elif c >= coarse - 2:
            n = c - (coarse - 2)
            size, base, side = (7 + n) * 32, 7 * 32 * n, 1
            at = rows - size
        else:
            full[c] = own_ref[c]
            continue
        one = first_ref[base : base + size, :].astype(F32)
        two = second_ref[base : base + size, :].astype(F32)
        extra = jnp.where(jnp.broadcast_to(odd == side, one.shape), two, one)
        if at > 0:
            full[c, 0:at, :] = own_ref[c, 0:at, :]
        if at + size < rows:
            full[c, at + size :, :] = own_ref[c, at + size :, :]
        full[c, at : at + size, :] = (own_ref[c, at : at + size, :].astype(F32) + extra).astype(BF16)
    for k, out_ref in enumerate(out_refs):
        target = jnp.bitwise_xor(me, k)
        row = jnp.int32(coarse)
        for c in range(coarse):
            row = jnp.where(owner_ref[0, me, c] == target, c, row)
        if len(out_refs) <= coarse:
            out_ref[...] = full[row]
        else:

            @pl.when(row < coarse)
            def _():
                out_ref[...] = full[row]

            @pl.when(row == coarse)
            def _():
                out_ref[...] = jnp.zeros(out_ref.shape, BF16)


def place_kernel(*refs):
    in_refs, out_ref, work = refs[:-2], refs[-2], refs[-1]
    count, (rows, _) = len(in_refs), in_refs[0].shape
    band = rows // 32
    pitch = 2 * rows + 1
    me = lax.axis_index("grp")
    for k, ref in enumerate(in_refs):
        at = jnp.bitwise_xor(me, k) * pitch
        work[pl.ds(at, rows, stride=2), :] = ref[...].astype(F32)

    def one(s, carry):
        for h in range(32):
            tile = work[pl.ds(s * 64 + 2 * h, count, stride=pitch), :]
            out_ref[s, :, h * 128 : (h + 1) * 128] = tile.astype(BF16)
        return carry

    lax.fori_loop(0, band, one, 0)


VM = pl.BlockSpec(memory_space=pltpu.VMEM)
SM = pl.BlockSpec(memory_space=pltpu.SMEM)
HBM = pl.BlockSpec(memory_space=pltpu.HBM)


def call(kernel, outs, ins, scratch=(), flops=0, size=0):
    return pl.pallas_call(
        kernel,
        out_shape=[jax.ShapeDtypeStruct(s, d) for s, d in outs],
        in_specs=ins,
        out_specs=[VM] * len(outs),
        scratch_shapes=list(scratch),
        compiler_params=pltpu.CompilerParams(vmem_limit_bytes=LIMIT),
        cost_estimate=pl.CostEstimate(flops=flops, bytes_accessed=size, transcendentals=0),
    )


def body(a_blocks, a_cols, p_blocks, p_cols, owner):
    rows, ka, width = a_blocks.shape
    group = p_cols.shape[0]
    coarse = rows // RATIO
    quads = rows // 8
    band = 11
    blks, grps = lax.axis_size("blk"), lax.axis_size("grp")
    cols_t = p_cols.T
    acols_t = a_cols.T
    p_flat = jnp.transpose(p_blocks, (1, 0, 2)).reshape(3 * rows, width)
    tail = width // 2 * 3
    (to_rows,) = call(
        send_rows_kernel, [((2, 8, tail), BF16)], [HBM, HBM],
        [pltpu.VMEM((3, group), jnp.int32), pltpu.VMEM((3 * rows, width), BF16), pltpu.SemaphoreType.DMA((2,))],
        size=1 << 20,
    )(cols_t, p_flat)
    pairs_a = [(i, i ^ 1) for i in range(blks)]
    pairs_b = [(i, ((i + 1) ^ 1) - 1) for i in range(blks)]
    pairs_b = [(i, j % blks) for i, j in pairs_b]
    p_first = lax.ppermute(to_rows[0], "blk", pairs_a)
    p_second = lax.ppermute(to_rows[1], "blk", pairs_b)
    lhs, z, pt, halo, base = call(
        merge_kernel,
        [((quads, 512, 1024), BF16), ((quads + 1, 512, 384), BF16), ((quads, 512, 384), BF16), ((2, 2, 2, 16, 16), BF16),
         ((2, 512, 512), F32)],
        [SM, HBM, HBM, HBM, HBM],
        [
            pltpu.VMEM((rows, ka, width), BF16),
            pltpu.VMEM((group, 128), F32),
            pltpu.SMEM((coarse,), jnp.int32),
            pltpu.SMEM((rows,), jnp.int32),
            pltpu.VMEM((quads, 128, 8 * ka), BF16),
            pltpu.VMEM(((quads + 1) * 32 + quads * 24, 6 * rows), BF16),
            pltpu.VMEM(((quads + 1) * 32 * 2 * (width // 64 + 1), 128), F32),
            pltpu.VMEM((6 * rows, width), BF16),
            pltpu.VMEM((6 * rows, width), BF16),
            pltpu.VMEM((3, group), jnp.int32),
            pltpu.VMEM((ka, rows), jnp.int32),
            pltpu.VMEM((3 * rows, width), BF16),
            pltpu.SemaphoreType.DMA((quads,)),
            pltpu.SemaphoreType.DMA((3,)),
        ],
        flops=4 << 30, size=16 << 20,
    )(cols_t, cols_t, acols_t, p_flat, a_blocks)
    sends, edge = call(
        edge_kernel,
        [((2, 15 * 32, 128), BF16), ((2, 512, 512), BF16)],
        [VM] * 6,
        [
            pltpu.VMEM((16 * 2 * (width // 64 + 1), 128), F32),
            pltpu.VMEM((2, 256, 384), BF16),
            pltpu.VMEM((4, 128, 128), F32),
        ],
        flops=1 << 30, size=4 << 20,
    )(halo, p_first, p_second, lhs, base, pt)
    from_first = lax.ppermute(sends[0], "blk", pairs_a)
    from_second = lax.ppermute(sends[1], "blk", pairs_b)
    (own,) = call(
        inner_kernel,
        [((coarse, band * 32, 128), BF16)],
        [VM] * 4,
        [pltpu.VMEM((quads + 3, coarse * 64, 128), F32), pltpu.VMEM((512, 512), BF16)],
        flops=2 << 30, size=8 << 20,
    )(lhs, z, pt, edge)
    outgoing = call(
        reduce_kernel, [((band * 32, 128), BF16)] * grps, [SM, VM, VM, VM],
        [pltpu.VMEM((coarse, band * 32, 128), BF16)], size=2 << 20,
    )(owner, own, from_first, from_second)
    arrived = [outgoing[0]] + [None] * (grps - 1)
    for k in range(grps - 1, 0, -1):
        arrived[k] = lax.ppermute(outgoing[k], "grp", [(i, i ^ k) for i in range(grps)])
    (placed,) = call(
        place_kernel, [((band, grps, width), BF16)], [VM] * grps,
        [pltpu.VMEM((grps * (2 * band * 32 + 1), 128), F32)], size=2 << 20,
    )(*arrived)
    return jnp.transpose(placed, (1, 0, 2))


def solution(mesh):
    return jax.shard_map(
        body,
        mesh=mesh,
        in_specs=(
            P(("grp", "blk"), None, None),
            P(("grp", "blk"), None),
            P(("grp", "blk"), None, None),
            P("grp", None),
            P("blk", None, None),
        ),
        out_specs=P(("grp", "blk"), None, None),
        check_vma=False,
    )
```

```python
import functools

import jax
import jax.numpy as jnp
from jax import lax
from jax.experimental import pallas as pl
from jax.experimental.pallas import tpu as pltpu
from jax.sharding import PartitionSpec as P

RATIO = 4
REACH = 2
F32 = jnp.float32
BF16 = jnp.bfloat16
LIMIT = 32 * 1024 * 1024
CHUNK = 4096
UNROLL = 1
PUNROLL = 8
ROWS = 512
ZUNROLL = 1


def iota(shape, axis):
    return lax.broadcasted_iota(jnp.int32, shape, axis)


def rows_sum(values):
    return jnp.sum(values.astype(F32), axis=0, keepdims=True)


def wrapped(values, modulus):
    half = modulus // 2
    values = jnp.where(values >= half, values - modulus, values)
    return jnp.where(values < -half, values + modulus, values)


def across(mask, values):
    picked = jnp.where(mask, values, 0.0).astype(BF16)
    return dot(picked, jnp.ones((picked.shape[1], 128), BF16))


def places(cols_ref, mine, rows):
    group = cols_ref.shape[1]
    agg_row = cols_ref[0:1, :].astype(F32)
    sub, lane = iota((group, group), 0), iota((group, group), 1)
    agg_wide = jnp.broadcast_to(agg_row, (group, group))
    agg_col = across(sub == lane, agg_wide)
    same = agg_wide == jnp.concatenate([agg_col] * (group // 128), axis=1)
    member_row = rows_sum(jnp.where(same & (sub < lane), 1.0, 0.0))
    member_col = across(same & (lane < sub), 1.0)
    base = (mine * rows).astype(F32)
    place_row = wrapped(agg_row * RATIO + member_row - base, group)
    place_col = wrapped(agg_col * RATIO + member_col - base, group)
    return place_row, place_col


def column_rel(cols_ref, mine, coarse):
    total = cols_ref.shape[1] // RATIO
    cols = cols_ref[...].astype(F32)
    near = wrapped(cols - cols[0:1, :], total)
    own = wrapped(cols[0:1, :] - (mine * coarse).astype(F32), total)
    return own + near


def own_lanes(values, mine, rows):
    group = values.shape[1]
    values = jnp.broadcast_to(values, (8, group))
    return pltpu.roll(values, (group - mine * rows) % group, 1)[:, :128]


def three_wide(pieces, rows):
    lane = iota((8, 128), 1)
    out = jnp.full((8, 128), -1.0, F32)
    for m, piece in enumerate(pieces):
        moved = piece if m == 0 else pltpu.roll(piece, m * rows, 1)
        out = jnp.where((lane >= m * rows) & (lane < (m + 1) * rows), moved, out)
    return out


def onehot(code, count):
    hit = iota((count, code.shape[1]), 0).astype(F32) == code
    return jnp.where(hit, 1.0, 0.0).astype(BF16)


def dot(a, b):
    return jnp.dot(a, b, preferred_element_type=F32)


def swap_halves(first, second):
    low = iota(first.shape, 1) < 64
    even = jnp.where(low, first, pltpu.roll(second, 64, 1))
    odd = jnp.where(low, pltpu.roll(first, 64, 1), second)
    return even, odd


def fetch(pairs, sems):
    copies = [pltpu.make_async_copy(src, dst, sems.at[n]) for n, (src, dst) in enumerate(pairs)]
    for copy in copies:
        copy.start()
    return copies


def send_rows_kernel(cols_hbm, p_hbm, acols_hbm, a_hbm, first_ref, second_ref, cols_ref, acols_ref, a_ref, pe, po,
                     work, p_ref, sems):
    copies = fetch(((cols_hbm, cols_ref), (p_hbm, p_ref), (acols_hbm, acols_ref), (a_hbm, a_ref)), sems)
    for copy in copies[:2]:
        copy.wait()
    rows = p_ref.shape[0] // 3
    width = p_ref.shape[1]
    half = width // 2
    mine = lax.axis_index("blk")
    place_row, _ = places(cols_ref, mine, rows)
    place = own_lanes(place_row, mine, rows)
    codes = [[], [], []]
    for first in (0, rows - RATIO):
        member = place - first
        good = (member >= 0) & (member < RATIO)
        none = jnp.full((8, 128), -1.0, F32)
        mem = jnp.where(good, member, none)
        nxt = jnp.where(good, member + RATIO, none)
        codes[0].append(three_wide((mem, nxt, none), rows))
        codes[1].append(three_wide((none, none, mem), rows))
        codes[2].append(three_wide((none, none, nxt), rows))
    picks = [jnp.concatenate([onehot(c[0:1, : 3 * rows], 8) for c in pair], axis=0) for pair in codes]
    work[:, :half] = dot(jnp.concatenate([picks[0], picks[1]], axis=0), p_ref[:, :half])
    work[:, half:] = dot(jnp.concatenate([picks[0], picks[2]], axis=0), p_ref[:, half:])
    odd = mine % 2
    for n, ref in enumerate((first_ref, second_ref)):
        at = pl.multiple_of((n + odd + 1) % 2 * 8, 8)
        last = pl.ds(16 + at, 8)
        ref[:, :half] = work[pl.ds(at, 8), :half].astype(BF16)
        ref[:, half:width] = work[pl.ds(at, 8), half:].astype(BF16)
        ref[:, width:] = (work[last, :half] + work[last, half:]).astype(BF16)
    p_rows = 3 * rows
    for at in range(0, width, 128):
        lanes = slice(at, at + 128)
        even, odds = halves(p_ref[:, lanes])
        for n in range(2):
            pe[n * p_rows : (n + 1) * p_rows, lanes] = even[n]
            po[n * p_rows : (n + 1) * p_rows, lanes] = odds[n]
    for copy in copies[2:]:
        copy.wait()


def halves(values):
    low = iota(values.shape, 1) % 128 < 64
    turned = jnp.concatenate(
        [pltpu.roll(values[:, at : at + 128], 64, 1) for at in range(0, values.shape[1], 128)], axis=1
    )
    none = jnp.zeros(values.shape, BF16)
    even = (jnp.where(low, values, none), jnp.where(low, none, turned))
    odd = (jnp.where(low, turned, none), jnp.where(low, none, values))
    return even, odd


def spread_store(flat, work_ref, row, pitch):
    for at in range(0, flat.shape[0], 8):
        work_ref[pl.ds(at * pitch + 2 * row, 8, stride=pitch), :] = flat[at : at + 8]


def spread_load(work_ref, j, pitch, out_ref, lead, at):
    size = pitch // 2 - 1
    for tile in range(3):
        block = work_ref[pl.ds((j * 4 + tile) * pitch, size, stride=2), :]
        out_ref[lead, pl.ds(at, size), tile * 128 : (tile + 1) * 128] = block.astype(BF16)


def unpack(values, ref, lead, at, pairs):
    for t in range(pairs):
        a, b = (
            jnp.concatenate([values[(2 * t + w) * 8 : (2 * t + w + 1) * 8, h * 128 : (h + 1) * 128]
                             for h in range(2)], axis=0).astype(BF16)
            for w in range(2)
        )
        even, odd = swap_halves(a, b)
        ref[lead, pl.ds(at, 16), t * 128 : (t + 1) * 128] = even
        ref[lead, pl.ds(at + 256, 16), t * 128 : (t + 1) * 128] = odd


def combine(low, high, at, put):
    put(at, 0, low[:, 0:128])
    put(at, 128, low[:, 128:] + high[:, :256])
    put(at, 384, high[:, 256:])


def merge_kernel(smem_cols, cols_ref, acols_ref, pe, po, a_ref, lhs_ref, z_ref, pt_ref, halo_ref, base_ref,
                 place_ref, count_smem, order_smem, sel, psel, work):
    rows, ka, width = a_ref.shape
    group = cols_ref.shape[1]
    coarse = rows // RATIO
    quads = rows // 8
    mine = lax.axis_index("blk")
    for c in range(coarse):
        count_smem[c] = 0
    for f in range(rows):
        agg = smem_cols[0, mine * rows + f] - mine * coarse
        at = count_smem[agg]
        count_smem[agg] = at + 1
        order_smem[agg * RATIO + at] = f
    p_rows = 3 * rows
    place_row, place_col = places(cols_ref, mine, rows)
    col_rel = column_rel(cols_ref, mine, coarse)
    first = ((mine - 1) * rows).astype(F32)

    step = 8 * ka
    span = quads * 256
    lane = iota((1, span), 1)
    inner = lane % 256
    lane_row = lane // 256 * 8 + inner // ka
    valid = inner < step
    rel = acols_ref[...].astype(F32) - first
    rel = jnp.where(rel < 0, rel + group, rel)
    rel = jnp.where(rel >= group, rel - group, rel)
    place_ref[...] = place_col
    own_col = place_ref[pl.ds(pl.multiple_of(mine * rows, 8), rows), :]
    own_col = jnp.concatenate([own_col] * (span // 128), axis=1)
    to_lane = jnp.where(own_col == jnp.where(valid, lane_row, -1).astype(F32), 1.0, 0.0).astype(BF16)
    wide = dot(rel.astype(BF16), to_lane)
    far = rows_sum(jnp.where(iota((ka, span), 0) == inner % ka, wide, 0.0))
    rel_w = iota((group, 128), 0).astype(F32) - first
    rel_w = jnp.where(rel_w < 0, rel_w + group, rel_w)
    rel_w = jnp.where(rel_w >= group, rel_w - group, rel_w)
    codes = []
    for at in range(0, span, 128):
        far_place = rows_sum(jnp.where(rel_w == far[:, at : at + 128], place_col, 0.0))
        codes.append(far_place)
    code = jnp.concatenate(codes, axis=1)
    code = (code - (8 * (lane // 256) - RATIO).astype(F32)) * 8 + (inner // ka).astype(F32)
    code = jnp.where(valid, code, -1.0)
    for q in range(quads):
        sel[q] = onehot(code[:, q * 256 : q * 256 + step], 128)

    place = own_lanes(place_row, mine, rows).astype(jnp.int32)
    z_rows, t_rows = (quads + 1) * 32, quads * 24
    codes = ([], []), ([], [])
    for m in range(3):
        col = own_lanes(col_rel[m : m + 1], mine, rows).astype(jnp.int32)
        pair, q = (place + RATIO) // 8, place // 8
        slot = col + 3 - 2 * pair
        z_code = pair * 32 + (place + RATIO) % 8 * 4 + slot // 2
        near = col + 2 - 2 * q
        t_code = q * 24 + near // 2 * 8 + place % 8
        for parity in range(2):
            codes[0][parity].append(jnp.where(slot % 2 == parity, z_code, -1).astype(F32))
            codes[1][parity].append(jnp.where(near % 2 == parity, t_code, -1).astype(F32))
    for parity in range(2):
        lanes = slice(parity * p_rows, (parity + 1) * p_rows)
        psel[0:z_rows, lanes] = onehot(three_wide(codes[0][parity], rows)[0:1, :p_rows], z_rows)
        psel[z_rows:, lanes] = onehot(three_wide(codes[1][parity], rows)[0:1, :p_rows], t_rows)

    diag = iota((group, group), 0) == iota((group, group), 1)
    col_cols = [across(diag, jnp.broadcast_to(col_rel[m : m + 1], (group, group)))[:, 0:16] for m in range(3)]
    place_16 = place_col[:, 0:16]
    r = iota((1, 16), 1)
    r_m = jnp.where(r < 8, r // RATIO, 2)
    r_i = r % RATIO
    for side, (start, shift) in enumerate(((-RATIO, 3), (rows, 3 - coarse))):
        hit = place_16 == (r_i + start).astype(F32)
        slot = jnp.zeros((1, 16), F32)
        for m in range(3):
            slot = jnp.where(r_m == m, rows_sum(jnp.where(hit, col_cols[m], 0.0)), slot)
        slot = slot.astype(jnp.int32) + shift
        row_code = r_i * 4 + slot // 2
        for part in range(2):
            keep = (r < 8) | (((r % 8) // RATIO) == part)
            for parity in range(2):
                code = jnp.where(keep & (slot % 2 == parity), row_code, -1).astype(F32)
                halo_ref[side, part, parity] = onehot(code, 16)

    pitch = 2 * (width // 64 + 1)

    def p_chunk(step, carry):
        lanes = pl.ds(pl.multiple_of(step * 256, 256), 256)
        for lo, ref in enumerate((pe, po)):
            picked = dot(psel[...], ref[:, lanes])
            for h in range(2):
                spread_store(picked[:z_rows, h * 128 : (h + 1) * 128], work, step * 4 + 2 * h + lo, pitch)
            for n in range(t_rows // 8):
                q, t = n // 3, n % 3
                rows8 = picked[z_rows + n * 8 : z_rows + n * 8 + 8]
                block = jnp.concatenate([rows8[:, :128], rows8[:, 128:]], axis=0).astype(BF16)
                pt_ref[q, pl.ds(pl.multiple_of(step * 16, 16) + 256 * lo, 16), t * 128 : (t + 1) * 128] = block
        return carry

    lax.fori_loop(0, width // 256, p_chunk, 0, unroll=PUNROLL)

    def z_pair(pair, carry):
        for j in range(8):
            spread_load(work, pair * 8 + j, pitch, z_ref, pair, j * 64)
        return carry

    lax.fori_loop(0, quads + 1, z_pair, 0, unroll=ZUNROLL)

    def quad(q, carry):
        def chunk(step, carry):
            lanes = pl.ds(pl.multiple_of(step * CHUNK, CHUNK), CHUNK)
            source = jnp.concatenate([a_ref[order_smem[q * 8 + i], :, lanes] for i in range(8)], axis=0)
            got = dot(sel[q], source)
            for h in range(CHUNK // 256):
                at = pl.multiple_of(step * (CHUNK // 16) + h * 16, 16)
                unpack(got[:, h * 256 : (h + 1) * 256], lhs_ref, q, at, 8)
            return carry

        return lax.fori_loop(0, width // CHUNK, chunk, carry, unroll=UNROLL)

    lax.fori_loop(0, quads, quad, 0)

    last = quads - 1
    for side, q in ((0, 0), (1, last)):

        def put(at, lane, value):
            base_ref[side, at : at + ROWS, lane : lane + value.shape[1]] = value

        for at in range(0, 512, ROWS):
            part = slice(at, at + ROWS)
            if side == 0:
                low = dot(lhs_ref[q, part, 256:512], z_ref[0, 256:512])
                high = dot(lhs_ref[q, part, 512:1024], z_ref[1])
            else:
                low = dot(lhs_ref[q, part, 0:512], z_ref[last])
                high = dot(lhs_ref[q, part, 512:768], z_ref[last + 1, 0:256])
            combine(low, high, at, put)


def second_product(pt, ap):
    return lax.dot_general(pt, ap, (((0,), (0,)), ((), ())), preferred_element_type=F32)


def blocks_of(acc_ref, row0, put):
    for tile in range(acc_ref.shape[0]):
        even = acc_ref[tile, pl.ds(row0, 32, stride=2), :]
        odd = acc_ref[tile, pl.ds(row0 + 1, 32, stride=2), :]
        first, second = swap_halves(even, odd)
        put(2 * tile, first)
        put(2 * tile + 1, second)


def edge_kernel(halo_ref, first_ref, second_ref, lhs_ref, base_ref, pt_ref, out_ref, ap_ref, work, zb, part):
    last = pt_ref.shape[0] - 1
    width = first_ref.shape[1] // 3 * 2
    half = width // 2
    odd = lax.axis_index("blk") % 2
    here = jnp.broadcast_to(odd, (8, 128)) == 0
    for side in range(2):
        def rows_of(lanes):
            one, two = first_ref[:, lanes].astype(F32), second_ref[:, lanes].astype(F32)
            even = jnp.broadcast_to(odd == side, one.shape)
            return jnp.where(even, two, one).astype(BF16)

        pitch = 2 * (width // 64 + 1)
        for h in range(2):
            rows16 = jnp.concatenate([rows_of(slice(h * half, (h + 1) * half)), rows_of(slice(width, None))], axis=0)
            for lo, stacks in enumerate(halves(rows16)):
                picked = dot(halo_ref[side, h, 0], stacks[0]) + dot(halo_ref[side, h, 1], stacks[1])
                for high in range(half // 128):
                    row = 2 * (h * (half // 128) + high) + lo
                    spread_store(picked[:, high * 128 : (high + 1) * 128], work, row, pitch)
        for j in range(4):
            spread_load(work, j, pitch, zb, side, j * 64)
    for side, q in ((0, 0), (1, last)):
        lane, more, lane0 = (0, 0, 0) if side == 0 else (768, 128, 384)
        for at in range(0, 512, 128):
            rows = slice(at, at + 128)
            extra = dot(lhs_ref[q, rows, lane : lane + 256], zb[side])
            ap_ref[side, rows, more : more + 384] = (base_ref[side, rows, more : more + 384] + extra).astype(BF16)
            ap_ref[side, rows, 384 - lane0 : 512 - lane0] = base_ref[side, rows, 384 - lane0 : 512 - lane0].astype(BF16)
        cut = slice(0, 128) if side == 0 else slice(256, 384)
        product = second_product(pt_ref[q, :, cut], ap_ref[side])
        for tile in range(4):
            part[tile] = product[:, tile * 128 : (tile + 1) * 128]
        target = out_ref.at[(side + odd + 1) % 2]
        for n, i in enumerate((0, 1) if side == 0 else (4, 5)):
            slots = range(4 - i, 11) if side == 0 else range(0, 12 - i)
            base = (0, 7)[n] if side == 0 else (0, 8)[n]

            def put(x, block):
                slot = x - i + 4
                if slot in slots:
                    at = (base + slot - slots[0]) * 32
                    target[at : at + 32, :] = block.astype(BF16)

            blocks_of(part, n * 64, put)


def inner_kernel(lhs_ref, z_ref, pt_ref, edge_ref, own_ref, acc, ap):
    quads = pt_ref.shape[0]
    coarse = own_ref.shape[0]
    band = own_ref.shape[1] // 32
    acc[...] = jnp.zeros(acc.shape, F32)
    for q in range(quads):
        if q == 0:
            product, at = second_product(pt_ref[q, :, 128:384], edge_ref[0]), 0
        elif q == quads - 1:
            product, at = second_product(pt_ref[q, :, 0:256], edge_ref[1]), acc.shape[1] - 256
        else:

            def put(at, lane, value):
                ap[at : at + 128, lane : lane + value.shape[1]] = value.astype(BF16)

            for at in range(0, 512, 128):
                rows = slice(at, at + 128)
                low = dot(lhs_ref[q, rows, 0:512], z_ref[q])
                high = dot(lhs_ref[q, rows, 512:1024], z_ref[q + 1])
                combine(low, high, at, put)
            product, at = second_product(pt_ref[q], ap[...]), (2 * q - 2) * 64
        for tile in range(4):
            acc[q + tile, at : at + product.shape[0], :] += product[:, tile * 128 : (tile + 1) * 128]
    for c in range(coarse):
        for slot in (s for s in range(band) if not 0 <= c + s - 2 < acc.shape[0] * 2):
            own_ref[c, slot * 32 : slot * 32 + 32, :] = jnp.zeros((32, 128), BF16)

        def put(x, block):
            slot = x - c + 2
            if 0 <= slot < band:
                own_ref[c, slot * 32 : slot * 32 + 32, :] = block.astype(BF16)

        blocks_of(acc, c * 64, put)


def reduce_kernel(owner_ref, own_ref, first_ref, second_ref, *refs):
    out_refs, full = refs[:-1], refs[-1]
    coarse, rows, _ = own_ref.shape
    me = lax.axis_index("grp")
    odd = lax.axis_index("blk") % 2
    for c in range(coarse):
        if c < 2:
            at, size, base, side = 0, (8 - c) * 32, 8 * 32 * c, 0
        elif c >= coarse - 2:
            n = c - (coarse - 2)
            size, base, side = (7 + n) * 32, 7 * 32 * n, 1
            at = rows - size
        else:
            full[c] = own_ref[c]
            continue
        one = first_ref[base : base + size, :].astype(F32)
        two = second_ref[base : base + size, :].astype(F32)
        extra = jnp.where(jnp.broadcast_to(odd == side, one.shape), two, one)
        if at > 0:
            full[c, 0:at, :] = own_ref[c, 0:at, :]
        if at + size < rows:
            full[c, at + size :, :] = own_ref[c, at + size :, :]
        full[c, at : at + size, :] = (own_ref[c, at : at + size, :].astype(F32) + extra).astype(BF16)
    for k, out_ref in enumerate(out_refs):
        target = jnp.bitwise_xor(me, k)
        row = jnp.int32(coarse)
        for c in range(coarse):
            row = jnp.where(owner_ref[0, me, c] == target, c, row)
        if len(out_refs) <= coarse:
            out_ref[...] = full[row]
        else:

            @pl.when(row < coarse)
            def _():
                out_ref[...] = full[row]

            @pl.when(row == coarse)
            def _():
                out_ref[...] = jnp.zeros(out_ref.shape, BF16)


def place_kernel(*refs):
    in_refs, out_ref, work = refs[:-2], refs[-2], refs[-1]
    count, (rows, _) = len(in_refs), in_refs[0].shape
    band = rows // 32
    pitch = 2 * rows + 1
    me = lax.axis_index("grp")
    for k, ref in enumerate(in_refs):
        at = jnp.bitwise_xor(me, k) * pitch
        work[pl.ds(at, rows, stride=2), :] = ref[...].astype(F32)

    def one(s, carry):
        for h in range(32):
            tile = work[pl.ds(s * 64 + 2 * h, count, stride=pitch), :]
            out_ref[s, :, h * 128 : (h + 1) * 128] = tile.astype(BF16)
        return carry

    lax.fori_loop(0, band, one, 0)


VM = pl.BlockSpec(memory_space=pltpu.VMEM)
SM = pl.BlockSpec(memory_space=pltpu.SMEM)
HBM = pl.BlockSpec(memory_space=pltpu.HBM)


def call(kernel, outs, ins, scratch=(), flops=0, size=0, limit=LIMIT):
    return pl.pallas_call(
        kernel,
        out_shape=[jax.ShapeDtypeStruct(s, d) for s, d in outs],
        in_specs=ins,
        out_specs=[VM] * len(outs),
        scratch_shapes=list(scratch),
        compiler_params=pltpu.CompilerParams(vmem_limit_bytes=limit),
        cost_estimate=pl.CostEstimate(flops=flops, bytes_accessed=size, transcendentals=0),
    )


def body(a_blocks, a_cols, p_blocks, p_cols, owner):
    rows, ka, width = a_blocks.shape
    group = p_cols.shape[0]
    coarse = rows // RATIO
    quads = rows // 8
    band = 11
    blks, grps = lax.axis_size("blk"), lax.axis_size("grp")
    cols_t = p_cols.T
    acols_t = a_cols.T
    p_flat = jnp.transpose(p_blocks, (1, 0, 2)).reshape(3 * rows, width)
    tail = width // 2 * 3
    ins = [pltpu.with_memory_space_constraint(x, pltpu.HBM) for x in (cols_t, p_flat, acols_t, a_blocks)]
    *to_rows, cols_v, acols_v, a_v, pe, po = call(
        send_rows_kernel,
        [((8, tail), BF16)] * 2 + [((3, group), jnp.int32), ((ka, rows), jnp.int32), ((rows, ka, width), BF16)]
        + [((6 * rows, width), BF16)] * 2,
        [HBM] * 4,
        [pltpu.VMEM((32, width), F32), pltpu.VMEM((3 * rows, width), BF16), pltpu.SemaphoreType.DMA((4,))],
        size=1 << 24, limit=20 << 20,
    )(*ins)
    pairs_a = [(i, i ^ 1) for i in range(blks)]
    pairs_b = [(i, ((i + 1) ^ 1) - 1) for i in range(blks)]
    pairs_b = [(i, j % blks) for i, j in pairs_b]
    p_first = lax.ppermute(to_rows[0], "blk", pairs_a)
    p_second = lax.ppermute(to_rows[1], "blk", pairs_b)
    lhs, z, pt, halo, base = call(
        merge_kernel,
        [((quads, 512, 1024), BF16), ((quads + 1, 512, 384), BF16), ((quads, 512, 384), BF16), ((2, 2, 2, 16, 16), BF16),
         ((2, 512, 512), F32)],
        [SM, VM, VM, VM, VM, VM],
        [
            pltpu.VMEM((group, 128), F32),
            pltpu.SMEM((coarse,), jnp.int32),
            pltpu.SMEM((rows,), jnp.int32),
            pltpu.VMEM((quads, 128, 8 * ka), BF16),
            pltpu.VMEM(((quads + 1) * 32 + quads * 24, 6 * rows), BF16),
            pltpu.VMEM(((quads + 1) * 32 * 2 * (width // 64 + 1), 128), F32),
        ],
        flops=4 << 30, size=16 << 20, limit=LIMIT,
    )(cols_v, cols_v, acols_v, pe, po, a_v)
    sends, edge = call(
        edge_kernel,
        [((2, 15 * 32, 128), BF16), ((2, 512, 512), BF16)],
        [VM] * 6,
        [
            pltpu.VMEM((16 * 2 * (width // 64 + 1), 128), F32),
            pltpu.VMEM((2, 256, 384), BF16),
            pltpu.VMEM((4, 128, 128), F32),
        ],
        flops=1 << 30, size=4 << 20,
    )(halo, p_first, p_second, lhs, base, pt)
    from_first = lax.ppermute(sends[0], "blk", pairs_a)
    from_second = lax.ppermute(sends[1], "blk", pairs_b)
    (own,) = call(
        inner_kernel,
        [((coarse, band * 32, 128), BF16)],
        [VM] * 4,
        [pltpu.VMEM((quads + 3, coarse * 64, 128), F32), pltpu.VMEM((512, 512), BF16)],
        flops=2 << 30, size=8 << 20,
    )(lhs, z, pt, edge)
    outgoing = call(
        reduce_kernel, [((band * 32, 128), BF16)] * grps, [SM, VM, VM, VM],
        [pltpu.VMEM((coarse, band * 32, 128), BF16)], size=2 << 20,
    )(owner, own, from_first, from_second)
    arrived = [outgoing[0]] + [None] * (grps - 1)
    for k in range(grps - 1, 0, -1):
        arrived[k] = lax.ppermute(outgoing[k], "grp", [(i, i ^ k) for i in range(grps)])
    (placed,) = call(
        place_kernel, [((band, grps, width), BF16)], [VM] * grps,
        [pltpu.VMEM((grps * (2 * band * 32 + 1), 128), F32)], size=2 << 20,
    )(*arrived)
    return jnp.transpose(placed, (1, 0, 2))


def solution(mesh):
    return jax.shard_map(
        body,
        mesh=mesh,
        in_specs=(
            P(("grp", "blk"), None, None),
            P(("grp", "blk"), None),
            P(("grp", "blk"), None, None),
            P("grp", None),
            P("blk", None, None),
        ),
        out_specs=P(("grp", "blk"), None, None),
        check_vma=False,
    )
```
